768 devices in a mesh: section: 24 (over z_lo, x, core), tp: 32 (over y, z_hi).
Axes of the slice: x: 4, y: 8, z: 12 (z_hi: 4, z_lo: 3; z = z_hi * 3 + z_lo), core: 2. Of those that a mesh axis runs over, the one named last changes fastest.
Arguments:
- inputs: bfloat16 [24, 128, 2560], P('section', 'tp'), may hold values from -6 to 6
- out_grad: bfloat16 [24, 128, 2560], P('section', 'tp'), may hold values from -6 to 6
- w_gate: bfloat16 [2560, 13824], P(None, 'tp'), may hold values from -0.125 to 0.125
- w_up: bfloat16 [2560, 13824], P(None, 'tp'), may hold values from -0.125 to 0.125
- w_down: bfloat16 [13824, 2560], P('tp'), may hold values from -0.125 to 0.125
Outputs:
- received: bfloat16 [24, 128, 2560], P('section', 'tp')
The draws below stay inside these ranges and needn't reach their ends.
All inputs are finite; a program needn't handle non-finite values.
Results may differ from the reference program's by a relative error of at most 0.0049.
Values may be sent and summed in bfloat16 or wider, within the bound.
No kernel may reach another device: no remote copies, remote signals or barrier semaphores. Data moves between devices by JAX's collectives and lax.ppermute only.
A program may use at most 32 MiB of HBM per device.

```python
import jax
import jax.numpy as jnp
from jax import lax

D = 2560
FF = 13824
TOKENS = 128
SECTIONS = 24


def shard_levels(rng, dims, split, low, high):
    def one(axis_at, shards_of):
        steps = jax.random.uniform(jax.random.fold_in(jax.random.fold_in(rng, 6), axis_at), (shards_of,), jnp.float32, low / len(split), high / len(split))
        return jnp.repeat(jnp.exp(steps), dims[axis_at] // shards_of).reshape((-1,) + (1,) * (len(dims) - axis_at - 1))

    loudness = one(*split[0])
    for cut in split[1:]:
        loudness = loudness * one(*cut)
    return loudness


def normal_values(key, shape, scale, most, cuts=(), kind=jnp.bfloat16):
    entries = scale * jax.random.normal(key, shape, jnp.float32)
    if cuts:
        entries = entries * shard_levels(key, shape, cuts, -0.22, 0.18)
    return jnp.clip(entries, -most, most).astype(kind)


def setup_inputs(seed: int = 0) -> dict:
    seeds = jax.random.split(jax.random.key(seed), 6)
    return {
        "inputs": normal_values(seeds[0], (SECTIONS, TOKENS, D), 1.0, 6.0, ((0, 24), (1, 32))),
        "out_grad": normal_values(seeds[1], (SECTIONS, TOKENS, D), 1.0, 6.0, ((0, 24), (1, 32))),
        "w_gate": normal_values(seeds[2], (D, FF), D ** -0.5, 0.125, ((1, 32),)),
        "w_up": normal_values(seeds[3], (D, FF), D ** -0.5, 0.125, ((1, 32),)),
        "w_down": normal_values(seeds[4], (FF, D), D ** -0.5, 0.125, ((0, 32),)),
    }


def one_section(args):
    inputs, out_grad, w_gate, w_up, w_down = args
    gate = jnp.dot(inputs, w_gate, preferred_element_type=jnp.float32)
    up = jnp.dot(inputs, w_up, preferred_element_type=jnp.float32)
    hid_grad = lax.dot_general(out_grad, w_down, (((1,), (1,)), ((), ())), preferred_element_type=jnp.float32)
    sig = jax.nn.sigmoid(gate)
    up_grad = (hid_grad * gate * sig).astype(jnp.bfloat16)
    gate_grad = (hid_grad * up * sig * (1.0 + gate * (1.0 - sig))).astype(jnp.bfloat16)
    total = lax.dot_general(gate_grad, w_gate, (((1,), (1,)), ((), ())), preferred_element_type=jnp.float32)
    total = total + lax.dot_general(up_grad, w_up, (((1,), (1,)), ((), ())), preferred_element_type=jnp.float32)
    return total.astype(jnp.bfloat16)


def reference(inputs, out_grad, w_gate, w_up, w_down):
    def step(pair):
        return one_section((pair[0], pair[1], w_gate, w_up, w_down))

    in_grad = lax.map(step, (inputs, out_grad))
    tail = jnp.zeros((1,) + in_grad.shape[1:], jnp.bfloat16)
    return jnp.concatenate([in_grad[1:], tail], axis=0)
```

```python
import jax
import jax.numpy as jnp
from jax import lax
from jax.sharding import Mesh, PartitionSpec as P

TP = ("y", "zh")


def passed_along(block, axis, distance):
    devices = range(lax.axis_size(axis))
    route = [(i - distance, i) for i in devices if i - distance in devices]
    return lax.ppermute(block, axis, route)


def on_device(inputs, out_grad, w_gate, w_up, w_down):
    rows, width = inputs.shape[1:]
    ny, nz = lax.axis_size("y"), lax.axis_size("zh")
    both = jnp.concatenate([inputs[0], out_grad[0]], axis=0)
    near = lax.all_to_all(
        jnp.broadcast_to(both, (nz,) + both.shape), "zh", 0, 0, tiled=True
    )
    near = near.reshape(nz, 2, rows, width).transpose(1, 0, 2, 3)
    near = near.reshape(2 * nz * rows, width)
    far = lax.all_to_all(
        jnp.broadcast_to(near, (ny,) + near.shape), "y", 0, 0, tiled=True
    )
    x = far[:, : nz * rows].reshape(-1, width)
    g = far[:, nz * rows :].reshape(-1, width)
    gate = jnp.dot(x, w_gate, preferred_element_type=jnp.float32)
    up = jnp.dot(x, w_up, preferred_element_type=jnp.float32)
    hid_grad = lax.dot_general(
        g, w_down, (((1,), (1,)), ((), ())), preferred_element_type=jnp.float32
    )
    sig = jax.nn.sigmoid(gate)
    up_grad = (hid_grad * gate * sig).astype(jnp.bfloat16)
    gate_grad = (hid_grad * up * sig * (1.0 + gate * (1.0 - sig))).astype(jnp.bfloat16)
    total = lax.dot_general(
        gate_grad, w_gate, (((1,), (1,)), ((), ())), preferred_element_type=jnp.float32
    ) + lax.dot_general(
        up_grad, w_up, (((1,), (1,)), ((), ())), preferred_element_type=jnp.float32
    )
    parts = total.astype(jnp.bfloat16).reshape(ny * nz, rows, width)
    parts = lax.all_to_all(parts, TP, 0, 0, tiled=True)
    in_grad = jnp.sum(parts.astype(jnp.float32), axis=0).astype(jnp.bfloat16)
    return passed_along(in_grad, "section", -1)[None]


def solution(mesh):
    n_section, n_tp = mesh.devices.shape
    fine = Mesh(mesh.devices.reshape(n_section, 8, n_tp // 8), ("section",) + TP)
    placed = (
        P("section", TP, None),
        P("section", TP, None),
        P(None, TP),
        P(None, TP),
        P(TP, None),
    )
    return jax.shard_map(
        on_device, mesh=fine, in_specs=placed, out_specs=P("section", TP, None), check_vma=False
    )
```

```python
import jax
import jax.numpy as jnp
from jax import lax
from jax.experimental import pallas as pl
from jax.experimental.pallas import tpu as pltpu
from jax.sharding import Mesh, PartitionSpec as P

TP = ("y", "zh")


def passed_along(block, axis, distance):
    devices = range(lax.axis_size(axis))
    route = [(i - distance, i) for i in devices if i - distance in devices]
    return lax.ppermute(block, axis, route)


def layer_kernel(far_ref, w_gate_ref, w_up_ref, w_down_hbm, out_ref, w_down_ref, arrived):
    fetch = pltpu.make_async_copy(w_down_hbm, w_down_ref, arrived)
    fetch.start()
    ny, both, width = far_ref.shape
    rows = both // 2
    nt = (((1,), (1,)), ((), ()))
    nn = (((1,), (0,)), ((), ()))
    x = far_ref[:, :rows, :].reshape(ny * rows, width)
    g = far_ref[:, rows:, :].reshape(ny * rows, width)
    gate = lax.dot_general(x, w_gate_ref[...], nt, preferred_element_type=jnp.float32)
    up = lax.dot_general(x, w_up_ref[...], nt, preferred_element_type=jnp.float32)
    fetch.wait()
    hid_grad = lax.dot_general(g, w_down_ref[...], nt, preferred_element_type=jnp.float32)
    sig = jax.nn.sigmoid(gate)
    hid_sig = hid_grad * sig
    up_grad = (hid_sig * gate).astype(jnp.bfloat16)
    gate_grad = (hid_sig * up * (1.0 + gate * (1.0 - sig))).astype(jnp.bfloat16)
    total = lax.dot_general(gate_grad, w_gate_ref[...], nn, preferred_element_type=jnp.float32)
    total = total + lax.dot_general(up_grad, w_up_ref[...], nn, preferred_element_type=jnp.float32)
    out_ref[...] = total.astype(jnp.bfloat16)


def hidden_and_back(far, w_gate, w_up, w_down):
    ny, both, width = far.shape
    hidden = w_gate.shape[0]
    tokens = ny * both // 2
    whole = pl.BlockSpec(memory_space=pltpu.VMEM)
    return pl.pallas_call(
        layer_kernel,
        out_shape=jax.ShapeDtypeStruct((tokens, width), jnp.bfloat16),
        in_specs=[whole] * 3 + [pl.BlockSpec(memory_space=pl.ANY)],
        out_specs=whole,
        scratch_shapes=[pltpu.VMEM(w_down.shape, w_down.dtype), pltpu.SemaphoreType.DMA],
        compiler_params=pltpu.CompilerParams(vmem_limit_bytes=16 * 2**20),
        cost_estimate=pl.CostEstimate(
            flops=10 * tokens * width * hidden,
            bytes_accessed=2 * (far.size + 3 * hidden * width + tokens * width),
            transcendentals=tokens * hidden,
        ),
    )(far, w_gate, w_up, w_down)


def on_device(inputs, out_grad, w_gate, w_up, w_down):
    rows, width = inputs.shape[1:]
    ny, nz = lax.axis_size("y"), lax.axis_size("zh")
    both = jnp.concatenate([inputs[0], out_grad[0]], axis=0)
    near = lax.all_to_all(
        jnp.broadcast_to(both, (nz,) + both.shape), "zh", 0, 0, tiled=True
    )
    near = near.reshape(nz, 2, rows, width).transpose(1, 0, 2, 3)
    near = near.reshape(2 * nz * rows, width)
    far = lax.all_to_all(
        jnp.broadcast_to(near, (ny,) + near.shape), "y", 0, 0, tiled=True
    )
    total = hidden_and_back(far, w_gate.T, w_up.T, w_down)
    parts = total.reshape(ny * nz, rows, width)
    parts = lax.all_to_all(parts, TP, 0, 0, tiled=True)
    in_grad = jnp.sum(parts.astype(jnp.float32), axis=0).astype(jnp.bfloat16)
    return passed_along(in_grad, "section", -1)[None]


def solution(mesh):
    n_section, n_tp = mesh.devices.shape
    fine = Mesh(mesh.devices.reshape(n_section, 8, n_tp // 8), ("section",) + TP)
    placed = (
        P("section", TP, None),
        P("section", TP, None),
        P(None, TP),
        P(None, TP),
        P(TP, None),
    )
    return jax.shard_map(
        on_device, mesh=fine, in_specs=placed, out_specs=P("section", TP, None), check_vma=False
    )
```

```python
import jax
import jax.numpy as jnp
from jax import lax
from jax.experimental import pallas as pl
from jax.experimental.pallas import tpu as pltpu
from jax.sharding import Mesh, PartitionSpec as P

TP = ("half", "odd", "zh")
JOINT = True


def handed_on(block, across, back):
    n, ny = lax.axis_size("section"), lax.axis_size("half") * lax.axis_size("odd")
    route = [
        (s * ny + y, (s - back) * ny + (y + (1 - 2 * ((y + s) % 2)) * across) % ny)
        for s in range(back, n)
        for y in range(ny)
    ]
    return lax.ppermute(block, ("section", "half", "odd"), route)


def layer_kernel(far_ref, w_gate_ref, w_up_ref, w_down_ref, out_ref):
    n, both, width = far_ref.shape
    rows = both // 2
    nt = (((1,), (1,)), ((), ()))
    nn = (((1,), (0,)), ((), ()))
    x = far_ref[:, :rows, :].reshape(n * rows, width)
    g = far_ref[:, rows:, :].reshape(n * rows, width)
    gate = lax.dot_general(x, w_gate_ref[...], nt, preferred_element_type=jnp.float32)
    up = lax.dot_general(x, w_up_ref[...], nt, preferred_element_type=jnp.float32)
    hid_grad = lax.dot_general(g, w_down_ref[...], nt, preferred_element_type=jnp.float32)
    sig = jax.nn.sigmoid(gate)
    hid_sig = hid_grad * sig
    up_grad = (hid_sig * gate).astype(jnp.bfloat16)
    gate_grad = (hid_sig * up * (1.0 + gate * (1.0 - sig))).astype(jnp.bfloat16)
    total = lax.dot_general(gate_grad, w_gate_ref[...], nn, preferred_element_type=jnp.float32)
    total = total + lax.dot_general(up_grad, w_up_ref[...], nn, preferred_element_type=jnp.float32)
    out_ref[...] = total.astype(out_ref.dtype)


def layer(far, w_gate, w_up, w_down, kind):
    n, both, width = far.shape
    hidden = w_gate.shape[0]
    tokens = n * both // 2
    whole = pl.BlockSpec(memory_space=pltpu.VMEM)
    return pl.pallas_call(
        layer_kernel,
        out_shape=jax.ShapeDtypeStruct((tokens, width), kind),
        in_specs=[whole] * 4,
        out_specs=whole,
        compiler_params=pltpu.CompilerParams(vmem_limit_bytes=16 * 2**20),
        cost_estimate=pl.CostEstimate(
            flops=10 * tokens * width * hidden,
            bytes_accessed=2 * (far.size + 3 * hidden * width + tokens * width),
            transcendentals=tokens * hidden,
        ),
    )(far, w_gate, w_up, w_down)


def on_device(inputs, out_grad, w_gate, w_up, w_down):
    rows, width = inputs.shape[1:]
    nh, nz = lax.axis_size("half"), lax.axis_size("zh")
    both = jnp.concatenate([inputs[0], out_grad[0]], axis=0)
    if JOINT:
        near = lax.all_to_all(
            jnp.broadcast_to(both, (nh * nz,) + both.shape), ("half", "zh"), 0, 0, tiled=True
        )
        own = near.reshape(nh, nz, 2, rows, width).transpose(0, 2, 1, 3, 4)
        own = own.reshape(nh, 2 * nz * rows, width)
    else:
        near = lax.all_to_all(
            jnp.broadcast_to(both, (nz,) + both.shape), "zh", 0, 0, tiled=True
        )
        near = near.reshape(nz, 2, rows, width).transpose(1, 0, 2, 3)
        near = near.reshape(2 * nz * rows, width)
        own = lax.all_to_all(
            jnp.broadcast_to(near, (nh,) + near.shape), "half", 0, 0, tiled=True
        )
    weights = (w_gate.T, w_up.T, w_down)
    other = handed_on(own, 1, 0)
    kept = layer(own, *weights, jnp.bfloat16)
    other, kept = lax.optimization_barrier((other, kept))
    kept = handed_on(kept, 0, 1)
    lent = layer(other, *weights, jnp.bfloat16)
    lent = handed_on(lent, 1, 1)
    total = kept.astype(jnp.float32) + lent.astype(jnp.float32)
    parts = total.astype(jnp.bfloat16).reshape(nh * nz, rows, width)
    parts = lax.all_to_all(parts, ("half", "zh"), 0, 0, tiled=True)
    in_grad = jnp.sum(parts.astype(jnp.float32), axis=0).astype(jnp.bfloat16)
    return in_grad[None]


def solution(mesh):
    n_section, n_tp = mesh.devices.shape
    fine = Mesh(mesh.devices.reshape(n_section, 4, 2, n_tp // 8), ("section",) + TP)
    placed = (
        P("section", TP, None),
        P("section", TP, None),
        P(None, TP),
        P(None, TP),
        P(TP, None),
    )
    return jax.shard_map(
        on_device, mesh=fine, in_specs=placed, out_specs=P("section", TP, None), check_vma=False
    )
```

```python
import jax
import jax.numpy as jnp
from jax import lax
from jax.experimental import pallas as pl
from jax.experimental.pallas import tpu as pltpu
from jax.sharding import Mesh, PartitionSpec as P

TP = ("half", "odd", "zh")
NT = (((1,), (1,)), ((), ()))
NN = (((1,), (0,)), ((), ()))
VMEM = pl.BlockSpec(memory_space=pltpu.VMEM)
PARAMS = pltpu.CompilerParams(vmem_limit_bytes=16 * 2**20)


def handed_on(block, across, back):
    n, ny = lax.axis_size("section"), lax.axis_size("half") * lax.axis_size("odd")
    route = [
        (s * ny + y, (s - back) * ny + (y + (1 - 2 * ((y + s) % 2)) * across) % ny)
        for s in range(back, n)
        for y in range(ny)
    ]
    return lax.ppermute(block, ("section", "half", "odd"), route)


def dot(a, b, dims):
    return lax.dot_general(a, b, dims, preferred_element_type=jnp.float32)


def sorted_rows(near_ref):
    n, eight, width = near_ref.shape
    pairs = near_ref[...].astype(jnp.float32).reshape(n // 2, 2, eight, width)
    even, odd = pairs[:, 0], pairs[:, 1]
    upper = lax.broadcasted_iota(jnp.int32, even.shape, 1) < eight // 2
    x = jnp.where(upper, even, pltpu.roll(odd, eight // 2, 1))
    g = jnp.where(upper, pltpu.roll(even, eight // 2, 1), odd)
    return [r.reshape(n * eight // 2, width).astype(near_ref.dtype) for r in (x, g)]


def gate_factors(gate, up):
    sig = jax.nn.sigmoid(gate)
    return up * sig * (1.0 + gate * (1.0 - sig)), gate * sig


def back(g, for_gate, for_up, w_gate, w_up, w_down):
    hid_grad = dot(g, w_down, NT)
    gate_grad = (hid_grad * for_gate).astype(jnp.bfloat16)
    up_grad = (hid_grad * for_up).astype(jnp.bfloat16)
    return dot(gate_grad, w_gate, NN) + dot(up_grad, w_up, NN)


def first_kernel(
    near_ref, w_gate_ref, w_up_hbm, w_down_hbm, out_ref, w_up_ref, w_down_ref, up_here, down_here
):
    up = pltpu.make_async_copy(w_up_hbm, w_up_ref, up_here)
    down = pltpu.make_async_copy(w_down_hbm, w_down_ref, down_here)
    up.start()
    down.start()
    x, g = sorted_rows(near_ref)
    gate = dot(x, w_gate_ref[...], NT)
    up.wait()
    factors = gate_factors(gate, dot(x, w_up_ref[...], NT))
    down.wait()
    total = back(g, *factors, w_gate_ref[...], w_up_ref[...], w_down_ref[...])
    out_ref[...] = total.astype(out_ref.dtype)


def cost(near, w_down):
    tokens = near.size // (2 * near.shape[-1])
    return pl.CostEstimate(
        flops=10 * tokens * w_down.size,
        bytes_accessed=6 * w_down.size + 2 * near.size,
        transcendentals=tokens * w_down.shape[0],
    )


def first(near, w_gate, w_up, w_down):
    tokens, width = near.size // (2 * near.shape[-1]), near.shape[-1]
    return pl.pallas_call(
        first_kernel,
        out_shape=[
            jax.ShapeDtypeStruct((tokens, width), near.dtype),
            jax.ShapeDtypeStruct(w_up.shape, w_up.dtype),
            jax.ShapeDtypeStruct(w_down.shape, w_down.dtype),
        ],
        in_specs=[VMEM] * 2 + [pl.BlockSpec(memory_space=pltpu.HBM)] * 2,
        out_specs=[VMEM] * 3,
        scratch_shapes=[pltpu.SemaphoreType.DMA] * 2,
        compiler_params=PARAMS,
        cost_estimate=cost(near, w_down),
    )(near, w_gate, *(pltpu.with_memory_space_constraint(w, pltpu.HBM) for w in (w_up, w_down)))


def second_kernel(near_ref, w_gate_ref, w_up_ref, w_down_ref, token_ref, out_ref):
    x, g = sorted_rows(near_ref)
    factors = gate_factors(dot(x, w_gate_ref[...], NT), dot(x, w_up_ref[...], NT))
    total = back(g, *factors, w_gate_ref[...], w_up_ref[...], w_down_ref[...])
    out_ref[...] = total.astype(out_ref.dtype)


def second(near, *operands):
    tokens, width = near.size // (2 * near.shape[-1]), near.shape[-1]
    return pl.pallas_call(
        second_kernel,
        out_shape=jax.ShapeDtypeStruct((tokens, width), near.dtype),
        in_specs=[VMEM] * (1 + len(operands)),
        out_specs=VMEM,
        compiler_params=PARAMS,
        cost_estimate=cost(near, operands[2]),
    )(near, *operands)


def turn_kernel(kept_ref, token_ref):
    token_ref[...] = kept_ref[: token_ref.shape[0], : token_ref.shape[1]].astype(token_ref.dtype)


def turn(kept):
    return pl.pallas_call(
        turn_kernel,
        out_shape=jax.ShapeDtypeStruct((8, 128), jnp.float32),
        in_specs=[VMEM],
        out_specs=VMEM,
        compiler_params=PARAMS,
    )(kept)


def on_device(inputs, out_grad, w_gate, w_up, w_down):
    rows, width = inputs.shape[1:]
    nh, nz = lax.axis_size("half"), lax.axis_size("zh")
    both = jnp.concatenate([inputs[0], out_grad[0]], axis=0)
    w_gate, w_up = w_gate.T, w_up.T
    near = lax.all_to_all(
        jnp.broadcast_to(both, (nh * nz,) + both.shape), ("half", "zh"), 0, 0, tiled=True
    )
    other = handed_on(near, 1, 0)
    kept, w_up, w_down = first(near, w_gate, w_up, w_down)
    sent = handed_on(kept, 0, 1)
    token = turn(kept)
    lent = second(other, w_gate, w_up, w_down, token)
    lent = handed_on(lent, 1, 1)
    total = sent.astype(jnp.float32) + lent.astype(jnp.float32)
    parts = total.astype(jnp.bfloat16).reshape(nh * nz, rows, width)
    parts = lax.all_to_all(parts, ("half", "zh"), 0, 0, tiled=True)
    in_grad = jnp.sum(parts.astype(jnp.float32), axis=0).astype(jnp.bfloat16)
    return in_grad[None]


def solution(mesh):
    n_section, n_tp = mesh.devices.shape
    fine = Mesh(mesh.devices.reshape(n_section, 4, 2, n_tp // 8), ("section",) + TP)
    placed = (
        P("section", TP, None),
        P("section", TP, None),
        P(None, TP),
        P(None, TP),
        P(TP, None),
    )
    return jax.shard_map(
        on_device, mesh=fine, in_specs=placed, out_specs=P("section", TP, None), check_vma=False
    )
```

```python
import jax
import jax.numpy as jnp
from jax import lax
from jax.experimental import pallas as pl
from jax.experimental.pallas import tpu as pltpu
from jax.sharding import Mesh, PartitionSpec as P

TP = ("half", "odd", "zh")
NT = (((1,), (1,)), ((), ()))
NN = (((1,), (0,)), ((), ()))
VMEM = pl.BlockSpec(memory_space=pltpu.VMEM)
PARAMS = pltpu.CompilerParams(vmem_limit_bytes=16 * 2**20)


def handed_on(block, across, back):
    n, ny = lax.axis_size("section"), lax.axis_size("half") * lax.axis_size("odd")
    route = [
        (s * ny + y, (s - back) * ny + (y + (1 - 2 * ((y + s) % 2)) * across) % ny)
        for s in range(back, n)
        for y in range(ny)
    ]
    return lax.ppermute(block, ("section", "half", "odd"), route)


def dot(a, b, dims):
    return lax.dot_general(a, b, dims, preferred_element_type=jnp.float32)


def sorted_rows(near_ref):
    n, both, width = near_ref.shape
    x, g = near_ref[:, : both // 2, :], near_ref[:, both // 2 :, :]
    return [r.reshape(n * both // 2, width) for r in (x, g)]


def gate_factors(gate, up):
    sig = jax.nn.sigmoid(gate)
    return up * sig * (1.0 + gate * (1.0 - sig)), gate * sig


def back(g, for_gate, for_up, w_gate, w_up, w_down):
    hid_grad = dot(g, w_down, NT)
    gate_grad = (hid_grad * for_gate).astype(jnp.bfloat16)
    up_grad = (hid_grad * for_up).astype(jnp.bfloat16)
    return dot(gate_grad, w_gate, NN) + dot(up_grad, w_up, NN)


def first_kernel(
    near_ref, w_gate_ref, w_up_hbm, w_down_hbm, out_ref, w_up_ref, w_down_ref, up_here, down_here
):
    up = pltpu.make_async_copy(w_up_hbm, w_up_ref, up_here)
    down = pltpu.make_async_copy(w_down_hbm, w_down_ref, down_here)
    up.start()
    down.start()
    x, g = sorted_rows(near_ref)
    gate = dot(x, w_gate_ref[...], NT)
    up.wait()
    factors = gate_factors(gate, dot(x, w_up_ref[...], NT))
    down.wait()
    total = back(g, *factors, w_gate_ref[...], w_up_ref[...], w_down_ref[...])
    out_ref[...] = total.astype(out_ref.dtype)


def cost(near, w_down):
    tokens = near.size // (2 * near.shape[-1])
    return pl.CostEstimate(
        flops=10 * tokens * w_down.size,
        bytes_accessed=6 * w_down.size + 2 * near.size,
        transcendentals=tokens * w_down.shape[0],
    )


def first(near, w_gate, w_up, w_down):
    tokens, width = near.size // (2 * near.shape[-1]), near.shape[-1]
    return pl.pallas_call(
        first_kernel,
        out_shape=[
            jax.ShapeDtypeStruct((tokens, width), near.dtype),
            jax.ShapeDtypeStruct(w_up.shape, w_up.dtype),
            jax.ShapeDtypeStruct(w_down.shape, w_down.dtype),
        ],
        in_specs=[VMEM] * 2 + [pl.BlockSpec(memory_space=pltpu.HBM)] * 2,
        out_specs=[VMEM] * 3,
        scratch_shapes=[pltpu.SemaphoreType.DMA] * 2,
        compiler_params=PARAMS,
        cost_estimate=cost(near, w_down),
    )(near, w_gate, *(pltpu.with_memory_space_constraint(w, pltpu.HBM) for w in (w_up, w_down)))


def second_kernel(near_ref, w_gate_ref, w_up_ref, w_down_ref, token_ref, out_ref):
    x, g = sorted_rows(near_ref)
    factors = gate_factors(dot(x, w_gate_ref[...], NT), dot(x, w_up_ref[...], NT))
    total = back(g, *factors, w_gate_ref[...], w_up_ref[...], w_down_ref[...])
    out_ref[...] = total.astype(out_ref.dtype)


def second(near, *operands):
    tokens, width = near.size // (2 * near.shape[-1]), near.shape[-1]
    return pl.pallas_call(
        second_kernel,
        out_shape=jax.ShapeDtypeStruct((tokens, width), near.dtype),
        in_specs=[VMEM] * (1 + len(operands)),
        out_specs=VMEM,
        compiler_params=PARAMS,
        cost_estimate=cost(near, operands[2]),
    )(near, *operands)


def turn_kernel(kept_ref, token_ref):
    token_ref[...] = kept_ref[: token_ref.shape[0], : token_ref.shape[1]].astype(token_ref.dtype)


def turn(kept):
    return pl.pallas_call(
        turn_kernel,
        out_shape=jax.ShapeDtypeStruct((8, 128), jnp.float32),
        in_specs=[VMEM],
        out_specs=VMEM,
        compiler_params=PARAMS,
    )(kept)


def on_device(inputs, out_grad, w_gate, w_up, w_down):
    rows, width = inputs.shape[1:]
    nh, nz = lax.axis_size("half"), lax.axis_size("zh")
    both = jnp.concatenate([inputs[0], out_grad[0]], axis=0)
    w_gate, w_up = w_gate.T, w_up.T
    close = lax.all_to_all(jnp.broadcast_to(both, (nz,) + both.shape), "zh", 0, 0, tiled=True)
    close = close.reshape(nz, 2, rows, width).transpose(1, 0, 2, 3)
    close = close.reshape(2 * nz * rows, width)
    near = lax.all_gather(close, "half", axis=0)
    other = handed_on(near, 1, 1)
    kept, w_up, w_down = first(near, w_gate, w_up, w_down)
    sent = handed_on(kept, 0, 1)
    token = turn(kept)
    lent = second(other, w_gate, w_up, w_down, token)
    lent = handed_on(lent, 1, 0)
    total = sent.astype(jnp.float32) + lent.astype(jnp.float32)
    parts = total.astype(jnp.bfloat16).reshape(nh * nz, rows, width)
    parts = lax.all_to_all(parts, ("half", "zh"), 0, 0, tiled=True)
    in_grad = jnp.sum(parts.astype(jnp.float32), axis=0).astype(jnp.bfloat16)
    return in_grad[None]


def solution(mesh):
    n_section, n_tp = mesh.devices.shape
    fine = Mesh(mesh.devices.reshape(n_section, 4, 2, n_tp // 8), ("section",) + TP)
    placed = (
        P("section", TP, None),
        P("section", TP, None),
        P(None, TP),
        P(None, TP),
        P(TP, None),
    )
    return jax.shard_map(
        on_device, mesh=fine, in_specs=placed, out_specs=P("section", TP, None), check_vma=False
    )
```

```python
import jax
import jax.numpy as jnp
from jax import lax
from jax.experimental import pallas as pl
from jax.experimental.pallas import tpu as pltpu
from jax.sharding import Mesh, PartitionSpec as P

TP = ("half", "odd", "zh")
NT = (((1,), (1,)), ((), ()))
NN = (((1,), (0,)), ((), ()))
VMEM = pl.BlockSpec(memory_space=pltpu.VMEM)
PARAMS = pltpu.CompilerParams(vmem_limit_bytes=16 * 2**20)


def handed_on(block, across, back):
    n, ny = lax.axis_size("section"), lax.axis_size("half") * lax.axis_size("odd")
    route = [
        (s * ny + y, (s - back) * ny + (y + (1 - 2 * ((y + s) % 2)) * across) % ny)
        for s in range(back, n)
        for y in range(ny)
    ]
    return lax.ppermute(block, ("section", "half", "odd"), route)


def dot(a, b, dims):
    return lax.dot_general(a, b, dims, preferred_element_type=jnp.float32)


def sorted_rows(near_ref):
    n, both, width = near_ref.shape
    x, g = near_ref[:, : both // 2, :], near_ref[:, both // 2 :, :]
    return [r.reshape(n * both // 2, width) for r in (x, g)]


def gate_factors(gate, up):
    sig = jax.nn.sigmoid(gate)
    return up * sig * (1.0 + gate * (1.0 - sig)), gate * sig


def back(g, for_gate, for_up, w_gate, w_up, w_down):
    hid_grad = dot(g, w_down, NT)
    gate_grad = (hid_grad * for_gate).astype(jnp.bfloat16)
    up_grad = (hid_grad * for_up).astype(jnp.bfloat16)
    return dot(gate_grad, w_gate, NN) + dot(up_grad, w_up, NN)


def first_kernel(
    near_ref, w_gate_ref, w_up_hbm, w_down_hbm, out_ref, w_up_ref, w_down_ref, up_here, down_here
):
    up = pltpu.make_async_copy(w_up_hbm, w_up_ref, up_here)
    down = pltpu.make_async_copy(w_down_hbm, w_down_ref, down_here)
    up.start()
    down.start()
    x, g = sorted_rows(near_ref)
    gate = dot(x, w_gate_ref[...], NT)
    up.wait()
    factors = gate_factors(gate, dot(x, w_up_ref[...], NT))
    down.wait()
    total = back(g, *factors, w_gate_ref[...], w_up_ref[...], w_down_ref[...])
    out_ref[...] = total.astype(out_ref.dtype)


def cost(near, w_down):
    tokens = near.size // (2 * near.shape[-1])
    return pl.CostEstimate(
        flops=10 * tokens * w_down.size,
        bytes_accessed=6 * w_down.size + 2 * near.size,
        transcendentals=tokens * w_down.shape[0],
    )


def first(near, w_gate, w_up, w_down):
    tokens, width = near.size // (2 * near.shape[-1]), near.shape[-1]
    return pl.pallas_call(
        first_kernel,
        out_shape=[
            jax.ShapeDtypeStruct((tokens, width), near.dtype),
            jax.ShapeDtypeStruct(w_up.shape, w_up.dtype),
            jax.ShapeDtypeStruct(w_down.shape, w_down.dtype),
        ],
        in_specs=[VMEM] * 2 + [pl.BlockSpec(memory_space=pltpu.HBM)] * 2,
        out_specs=[VMEM] * 3,
        scratch_shapes=[pltpu.SemaphoreType.DMA] * 2,
        compiler_params=PARAMS,
        cost_estimate=cost(near, w_down),
    )(near, w_gate, *(pltpu.with_memory_space_constraint(w, pltpu.HBM) for w in (w_up, w_down)))


def second_kernel(near_ref, w_gate_ref, w_up_ref, w_down_ref, token_ref, out_ref):
    x, g = sorted_rows(near_ref)
    factors = gate_factors(dot(x, w_gate_ref[...], NT), dot(x, w_up_ref[...], NT))
    total = back(g, *factors, w_gate_ref[...], w_up_ref[...], w_down_ref[...])
    out_ref[...] = total.astype(out_ref.dtype)


def second(near, *operands):
    tokens, width = near.size // (2 * near.shape[-1]), near.shape[-1]
    return pl.pallas_call(
        second_kernel,
        out_shape=jax.ShapeDtypeStruct((tokens, width), near.dtype),
        in_specs=[VMEM] * (1 + len(operands)),
        out_specs=VMEM,
        compiler_params=PARAMS,
        cost_estimate=cost(near, operands[2]),
    )(near, *operands)


def spread_kernel(inputs_hbm, out_grad_hbm, out_ref, inputs_ref, out_grad_ref, here):
    copies = [
        pltpu.make_async_copy(inputs_hbm, inputs_ref, here.at[0]),
        pltpu.make_async_copy(out_grad_hbm, out_grad_ref, here.at[1]),
    ]
    for c in copies:
        c.start()
    for c in copies:
        c.wait()
    parts = [r[0].astype(jnp.float32) for r in (inputs_ref, out_grad_ref)]
    both = jnp.concatenate(parts, axis=0).astype(out_ref.dtype)
    for i in range(out_ref.shape[0]):
        out_ref[i] = both


def spread(inputs, out_grad, copies):
    rows, width = inputs.shape[1:]
    return pl.pallas_call(
        spread_kernel,
        out_shape=jax.ShapeDtypeStruct((copies, 2 * rows, width), inputs.dtype),
        in_specs=[pl.BlockSpec(memory_space=pltpu.HBM)] * 2,
        out_specs=VMEM,
        scratch_shapes=[pltpu.VMEM(inputs.shape, inputs.dtype)] * 2
        + [pltpu.SemaphoreType.DMA((2,))],
        compiler_params=PARAMS,
    )(*(pltpu.with_memory_space_constraint(a, pltpu.HBM) for a in (inputs, out_grad)))


def turn_kernel(kept_ref, token_ref):
    token_ref[...] = kept_ref[: token_ref.shape[0], : token_ref.shape[1]].astype(token_ref.dtype)


def turn(kept):
    return pl.pallas_call(
        turn_kernel,
        out_shape=jax.ShapeDtypeStruct((8, 128), jnp.float32),
        in_specs=[VMEM],
        out_specs=VMEM,
        compiler_params=PARAMS,
    )(kept)


def on_device(inputs, out_grad, w_gate, w_up, w_down):
    rows, width = inputs.shape[1:]
    nh, nz = lax.axis_size("half"), lax.axis_size("zh")
    w_gate, w_up = w_gate.T, w_up.T
    close = lax.all_to_all(spread(inputs, out_grad, nz), "zh", 0, 0, tiled=True)
    close = close.reshape(nz, 2, rows, width).transpose(1, 0, 2, 3)
    close = close.reshape(2 * nz * rows, width)
    near = lax.all_gather(close, "half", axis=0)
    other = handed_on(near, 1, 1)
    kept, w_up, w_down = first(near, w_gate, w_up, w_down)
    sent = handed_on(kept, 0, 1)
    token = turn(kept)
    lent = second(other, w_gate, w_up, w_down, token)
    lent = handed_on(lent, 1, 0)
    total = sent.astype(jnp.float32) + lent.astype(jnp.float32)
    parts = total.astype(jnp.bfloat16).reshape(nh * nz, rows, width)
    parts = lax.all_to_all(parts, ("half", "zh"), 0, 0, tiled=True)
    in_grad = jnp.sum(parts.astype(jnp.float32), axis=0).astype(jnp.bfloat16)
    return in_grad[None]


def solution(mesh):
    n_section, n_tp = mesh.devices.shape
    fine = Mesh(mesh.devices.reshape(n_section, 4, 2, n_tp // 8), ("section",) + TP)
    placed = (
        P("section", TP, None),
        P("section", TP, None),
        P(None, TP),
        P(None, TP),
        P(TP, None),
    )
    return jax.shard_map(
        on_device, mesh=fine, in_specs=placed, out_specs=P("section", TP, None), check_vma=False
    )
```

```python
import jax
import jax.numpy as jnp
from jax import lax
from jax.experimental import pallas as pl
from jax.experimental.pallas import tpu as pltpu
from jax.sharding import Mesh, PartitionSpec as P

TP = ("half", "odd", "zh")
NT = (((1,), (1,)), ((), ()))
NN = (((1,), (0,)), ((), ()))
VMEM = pl.BlockSpec(memory_space=pltpu.VMEM)
PARAMS = pltpu.CompilerParams(vmem_limit_bytes=16 * 2**20)


def handed_on(block, across, back):
    n, ny = lax.axis_size("section"), lax.axis_size("half") * lax.axis_size("odd")
    route = [
        (s * ny + y, (s - back) * ny + (y + (1 - 2 * ((y + s) % 2)) * across) % ny)
        for s in range(back, n)
        for y in range(ny)
    ]
    return lax.ppermute(block, ("section", "half", "odd"), route)


def dot(a, b, dims):
    return lax.dot_general(a, b, dims, preferred_element_type=jnp.float32)


def sorted_rows(near_ref):
    n, both, width = near_ref.shape
    x, g = near_ref[:, : both // 2, :], near_ref[:, both // 2 :, :]
    return [r.reshape(n * both // 2, width) for r in (x, g)]


def gate_factors(gate, up):
    sig = jax.nn.sigmoid(gate)
    return up * sig * (1.0 + gate * (1.0 - sig)), gate * sig


def back(g, for_gate, for_up, w_gate, w_up, w_down):
    hid_grad = dot(g, w_down, NT)
    gate_grad = (hid_grad * for_gate).astype(jnp.bfloat16)
    up_grad = (hid_grad * for_up).astype(jnp.bfloat16)
    return dot(gate_grad, w_gate, NN) + dot(up_grad, w_up, NN)


def first_kernel(
    near_ref, w_gate_ref, w_up_hbm, w_down_hbm, out_ref, w_up_ref, w_down_ref, up_here, down_here
):
    up = pltpu.make_async_copy(w_up_hbm, w_up_ref, up_here)
    down = pltpu.make_async_copy(w_down_hbm, w_down_ref, down_here)
    up.start()
    down.start()
    x, g = sorted_rows(near_ref)
    gate = dot(x, w_gate_ref[...], NT)
    up.wait()
    factors = gate_factors(gate, dot(x, w_up_ref[...], NT))
    down.wait()
    total = back(g, *factors, w_gate_ref[...], w_up_ref[...], w_down_ref[...])
    out_ref[...] = total.astype(out_ref.dtype)


def cost(near, w_down):
    tokens = near.size // (2 * near.shape[-1])
    return pl.CostEstimate(
        flops=10 * tokens * w_down.size,
        bytes_accessed=6 * w_down.size + 2 * near.size,
        transcendentals=tokens * w_down.shape[0],
    )


def first(near, w_gate, w_up, w_down):
    tokens, width = near.size // (2 * near.shape[-1]), near.shape[-1]
    return pl.pallas_call(
        first_kernel,
        out_shape=[
            jax.ShapeDtypeStruct((tokens, width), near.dtype),
            jax.ShapeDtypeStruct(w_up.shape, w_up.dtype),
            jax.ShapeDtypeStruct(w_down.shape, w_down.dtype),
        ],
        in_specs=[VMEM] * 2 + [pl.BlockSpec(memory_space=pltpu.HBM)] * 2,
        out_specs=[VMEM] * 3,
        scratch_shapes=[pltpu.SemaphoreType.DMA] * 2,
        compiler_params=PARAMS,
        cost_estimate=cost(near, w_down),
    )(near, w_gate, *(pltpu.with_memory_space_constraint(w, pltpu.HBM) for w in (w_up, w_down)))


def second_kernel(near_ref, w_gate_ref, w_up_ref, w_down_ref, token_ref, out_ref):
    x, g = sorted_rows(near_ref)
    factors = gate_factors(dot(x, w_gate_ref[...], NT), dot(x, w_up_ref[...], NT))
    total = back(g, *factors, w_gate_ref[...], w_up_ref[...], w_down_ref[...])
    out_ref[...] = total.astype(out_ref.dtype)


def second(near, *operands):
    tokens, width = near.size // (2 * near.shape[-1]), near.shape[-1]
    return pl.pallas_call(
        second_kernel,
        out_shape=jax.ShapeDtypeStruct((tokens, width), near.dtype),
        in_specs=[VMEM] * (1 + len(operands)),
        out_specs=VMEM,
        compiler_params=PARAMS,
        cost_estimate=cost(near, operands[2]),
    )(near, *operands)


def spread_kernel(inputs_hbm, out_grad_hbm, out_ref, inputs_ref, out_grad_ref, here):
    copies = [
        pltpu.make_async_copy(inputs_hbm, inputs_ref, here.at[0]),
        pltpu.make_async_copy(out_grad_hbm, out_grad_ref, here.at[1]),
    ]
    for c in copies:
        c.start()
    for c in copies:
        c.wait()
    parts = [r[0].astype(jnp.float32) for r in (inputs_ref, out_grad_ref)]
    both = jnp.concatenate(parts, axis=0).astype(out_ref.dtype)
    for i in range(out_ref.shape[0]):
        out_ref[i] = both


def spread(inputs, out_grad, copies):
    rows, width = inputs.shape[1:]
    return pl.pallas_call(
        spread_kernel,
        out_shape=jax.ShapeDtypeStruct((copies, 2 * rows, width), inputs.dtype),
        in_specs=[pl.BlockSpec(memory_space=pltpu.HBM)] * 2,
        out_specs=VMEM,
        scratch_shapes=[pltpu.VMEM(inputs.shape, inputs.dtype)] * 2
        + [pltpu.SemaphoreType.DMA((2,))],
        compiler_params=PARAMS,
    )(*(pltpu.with_memory_space_constraint(a, pltpu.HBM) for a in (inputs, out_grad)))


def add_kernel(a_ref, b_ref, out_ref):
    total = a_ref[...].astype(jnp.float32) + b_ref[...].astype(jnp.float32)
    out_ref[...] = total.reshape(out_ref.shape).astype(out_ref.dtype)


def added(a, b, rows):
    tokens, width = a.shape
    return pl.pallas_call(
        add_kernel,
        out_shape=jax.ShapeDtypeStruct((tokens // rows, rows, width), a.dtype),
        in_specs=[VMEM] * 2,
        out_specs=VMEM,
        compiler_params=PARAMS,
    )(a, b)


def turn_kernel(kept_ref, token_ref):
    token_ref[...] = kept_ref[: token_ref.shape[0], : token_ref.shape[1]].astype(token_ref.dtype)


def turn(kept):
    return pl.pallas_call(
        turn_kernel,
        out_shape=jax.ShapeDtypeStruct((8, 128), jnp.float32),
        in_specs=[VMEM],
        out_specs=VMEM,
        compiler_params=PARAMS,
    )(kept)


def on_device(inputs, out_grad, w_gate, w_up, w_down):
    rows, width = inputs.shape[1:]
    nz = lax.axis_size("zh")
    w_gate, w_up = w_gate.T, w_up.T
    close = lax.all_to_all(spread(inputs, out_grad, nz), "zh", 0, 0, tiled=True)
    close = close.reshape(nz, 2, rows, width).transpose(1, 0, 2, 3)
    close = close.reshape(2 * nz * rows, width)
    near = lax.all_gather(close, "half", axis=0)
    other = handed_on(near, 1, 1)
    kept, w_up, w_down = first(near, w_gate, w_up, w_down)
    sent = handed_on(kept, 0, 1)
    token = turn(kept)
    lent = second(other, w_gate, w_up, w_down, token)
    lent = handed_on(lent, 1, 0)
    parts = added(sent, lent, rows)
    parts = lax.all_to_all(parts, ("half", "zh"), 0, 0, tiled=True)
    in_grad = jnp.sum(parts.astype(jnp.float32), axis=0).astype(jnp.bfloat16)
    return in_grad[None]


def solution(mesh):
    n_section, n_tp = mesh.devices.shape
    fine = Mesh(mesh.devices.reshape(n_section, 4, 2, n_tp // 8), ("section",) + TP)
    placed = (
        P("section", TP, None),
        P("section", TP, None),
        P(None, TP),
        P(None, TP),
        P(TP, None),
    )
    return jax.shard_map(
        on_device, mesh=fine, in_specs=placed, out_specs=P("section", TP, None), check_vma=False
    )
```
